32 devices in a mesh: dp: 8 (over z, x), expert: 4 (over y, core).
Axes of the slice: x: 2, y: 2, z: 4, core: 2. Of those that a mesh axis runs over, the one named last changes fastest.
Arguments:
- tokens: bfloat16 [6272, 768], P(('dp', 'expert')), may hold values from -6 to 6
- counts: int32 [32, 2], P(('dp', 'expert')), may hold values from 0 to 4, as said below
- routes: int32 [6272, 2], P(('dp', 'expert')), may hold values from 0 to 31, all different within a row
- priority: int32 [32, 196], P(('dp', 'expert')), may hold values from 0 to 195, each once within a row
- out_grad: bfloat16 [6272, 768], P(('dp', 'expert')), may hold values from -6 to 6
- pre_gain: bfloat16 [768], P(('dp', 'expert')), may hold values from 0.5 to 1.5
- pre_shift: bfloat16 [768], P(('dp', 'expert')), may hold values from -1.5 to 1.5
- w_qkv: bfloat16 [768, 2304], P(('dp', 'expert')), may hold values from -0.21875 to 0.21875
- w_out: bfloat16 [768, 768], P(('dp', 'expert')), may hold values from -0.625 to 0.625
- moe_gain: bfloat16 [768], P(('dp', 'expert')), may hold values from 0.5 to 1.5
- moe_shift: bfloat16 [768], P(('dp', 'expert')), may hold values from -1.5 to 1.5
- w_router: bfloat16 [768, 32], P(('dp', 'expert')), may hold values from -0.15625 to 0.15625
- w_up: bfloat16 [32, 768, 3072], P('expert', 'dp'), may hold values from -0.21875 to 0.21875
- w_down: bfloat16 [32, 3072, 768], P('expert', 'dp'), may hold values from -0.109375 to 0.109375
Outputs:
- out_tokens: bfloat16 [6272, 768], P(('dp', 'expert'))
- d_tokens: float32 [6272, 768], P(('dp', 'expert'))
- d_pre_gain: float32 [768], P(('dp', 'expert'))
- d_pre_shift: float32 [768], P(('dp', 'expert'))
- d_w_qkv: float32 [768, 2304], P(('dp', 'expert'))
- d_w_out: float32 [768, 768], P(('dp', 'expert'))
- d_moe_gain: float32 [768], P(('dp', 'expert'))
- d_moe_shift: float32 [768], P(('dp', 'expert'))
- d_w_router: float32 [768, 32], P(('dp', 'expert'))
- d_w_up: float32 [32, 768, 3072], P('expert', 'dp')
- d_w_down: float32 [32, 3072, 768], P('expert', 'dp')
The draws below stay inside these ranges and needn't reach their ends.
Inputs may be any that keep to these rules, and one draw needn't show every extreme that they name: counts[s,0] is the number of large images (196 patches) and counts[s,1] of small ones (49 patches) of shard s, laid from the shard's first row, large ones first; counts[s,1] = (196 - 196 counts[s,0]) // 49; counts[s,0] is at most 1. `routes`: the two experts of a row differ. Each row of priority names every rank once; lower ranks take slots first.
All inputs are finite; a program needn't handle non-finite values.
Results may differ from the reference program's by a relative error of at most 0.014.
Values may be sent and summed in bfloat16 or wider, within the bound.
A program may use at most 320 MiB of HBM per device.

```python
import math
import jax
import jax.numpy as jnp
from jax import lax

D = 768
HEADS = 12
HEAD_DIM = 64
FF = 3072
EXPERTS = 32
PATCH_S = 49
PATCH_L = 196
LARGE_MAX = 1
TOK_DEV = 196
CAP = 13
SHARDS = 32
TOKENS = 6272


def draw_counts(key, part):
    order = jax.random.permutation(key, SHARDS)
    large_count = order % (LARGE_MAX + 1)
    small_count = (TOK_DEV - PATCH_L * large_count) // PATCH_S
    return jnp.stack([large_count, small_count], axis=1).astype(jnp.int32)


def steps_of(key, extent, shards, low, top_value):
    loudness = 1.0
    for dim, blocks in shards:
        steps = jax.random.uniform(jax.random.fold_in(jax.random.fold_in(key, 6), dim), (blocks,), jnp.float32, low / len(shards), top_value / len(shards))
        loudness = loudness * jnp.repeat(jnp.exp(steps), extent[dim] // blocks).reshape((-1,) + (1,) * (len(extent) - 1 - dim))
    return loudness


def distinct(stream_key, rows, amount, top, lift):
    order = jax.random.permutation(jax.random.fold_in(stream_key, 1), amount)
    boost = order
    for power in range(3):
        boost = boost * boost // amount
    boost = boost * lift // amount
    lots = jax.random.randint(jax.random.fold_in(stream_key, 2), (rows, amount), 0, 4096) + boost
    fixed_rows = jax.random.permutation(jax.random.fold_in(stream_key, 3), rows)[jnp.arange(amount) % rows]
    lots = jnp.where(jnp.arange(rows)[:, None] == fixed_rows[None, :], 1 << 14, lots)
    score = lots * amount + jnp.arange(amount)
    return lax.top_k(score.astype(jnp.int32), top)[1].astype(jnp.int32)


def scatter_about(key, dims, width, bound, shards=(), kind=jnp.bfloat16):
    loudness = steps_of(key, dims, shards, -0.22, 0.18) if shards else 1.0
    drawn = jax.random.normal(key, dims, jnp.float32) * width * loudness
    return jnp.minimum(jnp.maximum(drawn, -bound), bound).astype(kind)


def setup_inputs(seed: int = 0) -> dict:
    key_list = jax.random.split(jax.random.key(seed), 15)
    tokens = scatter_about(key_list[0], (TOKENS, D), 1.0, 6.0, ((0, 32),))
    counts = draw_counts(jax.random.fold_in(key_list[14], 71), 0)
    routes = distinct(key_list[2], TOKENS, EXPERTS, 2, 512)
    priority = jax.vmap(lambda own: jax.random.permutation(own, TOK_DEV))(jax.random.split(key_list[3], SHARDS)).reshape((SHARDS, TOK_DEV)).astype(jnp.int32)
    out_grad = scatter_about(key_list[4], (TOKENS, D), 1.0, 6.0, ((0, 32),))
    pre_gain = jnp.clip(1.0 + 0.1 * jax.random.normal(key_list[5], (D,), jnp.float32), 0.5, 1.5).astype(jnp.bfloat16)
    pre_shift = scatter_about(key_list[6], (D,), 0.3, 1.5, ((0, 32),))
    w_qkv = scatter_about(key_list[7], (D, 3 * D), D ** -0.5, 0.21875, ((0, 32),))
    w_out = scatter_about(key_list[8], (D, D), (D // 8) ** -0.5, 0.625, ((0, 32),))
    moe_gain = jnp.clip(1.0 + 0.1 * jax.random.normal(key_list[9], (D,), jnp.float32), 0.5, 1.5).astype(jnp.bfloat16)
    moe_shift = scatter_about(key_list[10], (D,), 0.3, 1.5, ((0, 32),))
    w_router = scatter_about(key_list[11], (D, EXPERTS), (2 * D) ** -0.5, 0.15625, ((0, 32),))
    w_up = scatter_about(key_list[12], (EXPERTS, D, FF), D ** -0.5, 0.21875, ((0, 4), (1, 8)))
    w_down = scatter_about(key_list[13], (EXPERTS, FF, D), FF ** -0.5, 0.109375, ((0, 4), (1, 8)))
    return dict(tokens=tokens, counts=counts, routes=routes, priority=priority, out_grad=out_grad, pre_gain=pre_gain, pre_shift=pre_shift, w_qkv=w_qkv, w_out=w_out, moe_gain=moe_gain, moe_shift=moe_shift, w_router=w_router, w_up=w_up, w_down=w_down)


HIGHEST = lax.Precision.HIGHEST

@jax.custom_vjp
def low(v):
    return lax.optimization_barrier(v.astype(jnp.bfloat16)).astype(jnp.float32)

@jax.custom_vjp
def low_back(v):
    return v

def low_keep(v):
    return (low(v), None)

def low_pass(kept, grad):
    return (grad,)

def back_keep(v):
    return (v, None)

def back_low(kept, grad):
    return (low(grad),)
low.defvjp(low_keep, low_pass)
low_back.defvjp(back_keep, back_low)

def normalize(inputs, scale_vec, shift_vec):
    average = lax.optimization_barrier(jnp.mean(inputs, axis=-1, keepdims=True))
    centred = inputs - average
    variance = lax.optimization_barrier(jnp.mean(centred * centred, axis=-1, keepdims=True))
    return centred * lax.rsqrt(variance + 1e-06) * scale_vec + shift_vec

def slot_numbers(chosen, rank_of, usable):
    earlier = (rank_of[:, None] < rank_of[None, :]) & usable[:, None]
    first_ids = chosen[:, 0]
    second_ids = chosen[:, 1]
    slot_first = lax.optimization_barrier(jnp.sum((earlier & (first_ids[:, None] == first_ids[None, :])).astype(jnp.int32), axis=0))
    crossing = usable[:, None] & (first_ids[:, None] == second_ids[None, :])
    slot_second = lax.optimization_barrier(jnp.sum((earlier & (second_ids[:, None] == second_ids[None, :])).astype(jnp.int32), axis=0))
    slot_second = slot_second + lax.optimization_barrier(jnp.sum(crossing.astype(jnp.int32), axis=0))
    return jnp.stack([slot_first, slot_second], axis=1)

def slot_shard(operands):
    return slot_numbers(operands[0], operands[1], operands[2])

def attention_shard(normed, segment_row, qkv_mat, out_mat):
    row_count = normed.shape[0]
    projected = low(low_back(jnp.dot(low(normed), qkv_mat, precision=HIGHEST)))
    queries = projected[:, :D].reshape(row_count, HEADS, HEAD_DIM)
    key_rows = projected[:, D:2 * D].reshape(row_count, HEADS, HEAD_DIM)
    value_rows = projected[:, 2 * D:].reshape(row_count, HEADS, HEAD_DIM)
    raw_scores = low_back(jnp.einsum('qhc,khc->hqk', queries, key_rows, precision=HIGHEST))
    same_seg = (segment_row[:, None] == segment_row[None, :])[None]
    attn_probs = jax.nn.softmax(jnp.where(same_seg, raw_scores * (1.0 / math.sqrt(HEAD_DIM)), -1e+30), axis=-1)
    mixed_rows = jnp.einsum('hqk,khc->qhc', low(attn_probs), value_rows, precision=HIGHEST).reshape(row_count, D)
    return low_back(jnp.dot(low(low_back(mixed_rows)), out_mat, precision=HIGHEST))

def reference(tokens, counts, routes, priority, out_grad, pre_gain, pre_shift, w_qkv, w_out, moe_gain, moe_shift, w_router, w_up, w_down):
    positions = jnp.arange(TOK_DEV, dtype=jnp.int32)[None, :]
    large_count = counts[:, 0:1]
    small_count = counts[:, 1:2]
    large_end = large_count * PATCH_L
    used_end = large_end + small_count * PATCH_S
    segment_ids = jnp.where(positions < large_end, positions // PATCH_L, jnp.where(positions < used_end, large_count + (positions - large_end) // PATCH_S, -1)).astype(jnp.int32)
    usable = positions < used_end
    chosen = routes.reshape(SHARDS, TOK_DEV, 2)
    slot_ids = lax.map(slot_shard, (chosen, priority, usable))
    kept_mask = usable[:, :, None] & (slot_ids < CAP)
    shard_ids = jnp.arange(SHARDS, dtype=jnp.int32)[:, None, None]
    rows_all = SHARDS * CAP
    flat_dest = jnp.where(kept_mask, chosen * rows_all + shard_ids * CAP + slot_ids, EXPERTS * rows_all).astype(jnp.int32).reshape(TOKENS, 2)
    token_ids = jnp.repeat(jnp.arange(TOKENS, dtype=jnp.int32), 2)
    source_table = jnp.full((EXPERTS * rows_all + 1,), TOKENS, jnp.int32).at[flat_dest.reshape(-1)].set(token_ids)
    source_table = source_table[:EXPERTS * rows_all].reshape(EXPERTS, rows_all)

    def forward(tokens_f, pre_gain_f, pre_shift_f, qkv_f, out_f, moe_gain_f, moe_shift_f, router_f, up_f, down_f):
        grouped = tokens_f.reshape(SHARDS, TOK_DEV, D)

        def attend(operands):
            rows_in = operands[0]
            return rows_in + attention_shard(normalize(rows_in, pre_gain_f, pre_shift_f), operands[1], qkv_f, out_f)
        middle = lax.map(jax.checkpoint(attend), (grouped, segment_ids)).reshape(TOKENS, D)
        normed_two = low(normalize(middle, moe_gain_f, moe_shift_f))
        logits = jnp.dot(normed_two, router_f, precision=HIGHEST)
        picked = jnp.take_along_axis(logits, routes, axis=1)
        gate_vals = jax.nn.softmax(picked, axis=-1)
        padded = jnp.concatenate([normed_two, jnp.zeros((1, D), jnp.float32)], axis=0)

        def expert_fn(operands):
            inputs = low_back(jnp.take(padded, operands[0], axis=0))
            hidden = low_back(jnp.dot(inputs, operands[1], precision=HIGHEST))
            activated = low(jax.nn.gelu(hidden, approximate=False))
            return low(low_back(jnp.dot(activated, operands[2], precision=HIGHEST)))
        outputs = lax.map(jax.checkpoint(expert_fn), (source_table, up_f, down_f))
        stacked = jnp.concatenate([outputs.reshape(EXPERTS * rows_all, D), jnp.zeros((1, D), jnp.float32)], axis=0)
        mixture = gate_vals[:, 0:1] * jnp.take(stacked, flat_dest[:, 0], axis=0)
        mixture = mixture + gate_vals[:, 1:2] * jnp.take(stacked, flat_dest[:, 1], axis=0)
        return middle + mixture
    floats = tuple((array.astype(jnp.float32) for array in (tokens, pre_gain, pre_shift, w_qkv, w_out, moe_gain, moe_shift, w_router, w_up, w_down)))
    result, pullback = jax.vjp(forward, *floats)
    gradients = pullback(out_grad.astype(jnp.float32))
    return (result.astype(jnp.bfloat16), gradients[0], gradients[1], gradients[2], gradients[3], gradients[4], gradients[5], gradients[6], gradients[7], gradients[8], gradients[9])
```

```python
from functools import partial
import math

import jax
import jax.numpy as jnp
from jax import lax
from jax.sharding import PartitionSpec as P

D = 768
HEADS = 12
HEAD_DIM = 64
EXPERTS = 32
PATCH_S = 49
PATCH_L = 196
CAP = 13


def normalize(inputs, scale_vec, shift_vec):
    average = jnp.mean(inputs, axis=-1, keepdims=True)
    centred = inputs - average
    variance = jnp.mean(centred * centred, axis=-1, keepdims=True)
    return centred * lax.rsqrt(variance + 1e-06) * scale_vec + shift_vec


def slot_numbers(chosen, rank_of, usable):
    earlier = (rank_of[:, None] < rank_of[None, :]) & usable[:, None]
    first_ids = chosen[:, 0]
    second_ids = chosen[:, 1]
    slot_first = jnp.sum(
        (earlier & (first_ids[:, None] == first_ids[None, :])).astype(jnp.int32), axis=0
    )
    crossing = usable[:, None] & (first_ids[:, None] == second_ids[None, :])
    slot_second = jnp.sum(
        (earlier & (second_ids[:, None] == second_ids[None, :])).astype(jnp.int32), axis=0
    )
    slot_second = slot_second + jnp.sum(crossing.astype(jnp.int32), axis=0)
    return jnp.stack([slot_first, slot_second], axis=1)


def block_probs(query_blk, seg_blk, key_rows, segment_ids):
    raw_scores = jnp.einsum("qhc,khc->hqk", query_blk, key_rows, preferred_element_type=jnp.float32)
    same_seg = (seg_blk[:, None] == segment_ids[None, :])[None]
    return jax.nn.softmax(
        jnp.where(same_seg, raw_scores * (1.0 / math.sqrt(HEAD_DIM)), -1e30), axis=-1
    )


def body(
    tokens,
    counts,
    routes,
    priority,
    out_grad,
    pre_gain,
    pre_shift,
    w_qkv,
    w_out,
    moe_gain,
    moe_shift,
    w_router,
    w_up,
    w_down,
):
    every = ("dp", "expert")
    dense = lax.all_gather(
        jnp.concatenate(
            [w_qkv, w_out, w_router]
            + [vector[:, None] for vector in (pre_gain, pre_shift, moe_gain, moe_shift)],
            axis=1,
        ),
        every,
        axis=0,
        tiled=True,
    )
    edges = (3 * D, 4 * D, 4 * D + EXPERTS)
    qkv_full, outp_full, router_full = (
        dense[:, : edges[0]],
        dense[:, edges[0] : edges[1]],
        dense[:, edges[1] : edges[2]],
    )
    gain_one, shift_one, gain_two, shift_two = (dense[:, edges[2] + i] for i in range(4))
    up_slice = lax.all_to_all(w_up, "dp", split_axis=2, concat_axis=1, tiled=True)
    row_count = tokens.shape[0]
    scale_factor = 1.0 / math.sqrt(HEAD_DIM)
    positions = jnp.arange(row_count, dtype=jnp.int32)
    large_count = counts[0, 0]
    small_count = counts[0, 1]
    large_end = large_count * PATCH_L
    used_end = large_end + small_count * PATCH_S
    segment_ids = jnp.where(
        positions < large_end,
        positions // PATCH_L,
        jnp.where(positions < used_end, large_count + (positions - large_end) // PATCH_S, -1),
    )
    usable = positions < used_end
    rows_in = tokens.astype(jnp.float32)
    normed_one, pull_one = jax.vjp(
        normalize, rows_in, gain_one.astype(jnp.float32), shift_one.astype(jnp.float32)
    )
    packed_one = normed_one.astype(jnp.bfloat16)
    projected = jnp.dot(packed_one, qkv_full, preferred_element_type=jnp.float32).astype(
        jnp.bfloat16
    )
    queries = projected[:, :D].reshape(row_count, HEADS, HEAD_DIM)
    key_rows = projected[:, D : 2 * D].reshape(row_count, HEADS, HEAD_DIM)
    value_rows = projected[:, 2 * D :].reshape(row_count, HEADS, HEAD_DIM)
    blocks = row_count // PATCH_L
    query_blocks = queries.reshape(blocks, PATCH_L, HEADS, HEAD_DIM)
    seg_blocks = segment_ids.reshape(blocks, PATCH_L)

    def forward_block(operands):
        attn_probs = block_probs(operands[0], operands[1], key_rows, segment_ids)
        return jnp.einsum(
            "hqk,khc->qhc",
            attn_probs.astype(jnp.bfloat16),
            value_rows,
            preferred_element_type=jnp.float32,
        ).astype(jnp.bfloat16)

    mixed_rows = lax.map(forward_block, (query_blocks, seg_blocks)).reshape(row_count, D)
    middle = rows_in + jnp.dot(mixed_rows, outp_full, preferred_element_type=jnp.float32)
    normed_two, pull_two = jax.vjp(
        normalize, middle, gain_two.astype(jnp.float32), shift_two.astype(jnp.float32)
    )
    packed_two = normed_two.astype(jnp.bfloat16)
    router_f32 = router_full.astype(jnp.float32)
    packed_f32 = packed_two.astype(jnp.float32)
    logits = jnp.dot(packed_two, router_full, preferred_element_type=jnp.float32)
    expert_ids = jnp.arange(EXPERTS, dtype=jnp.int32)
    onehot = routes[:, :, None] == expert_ids[None, None, :]
    picked = jnp.sum(jnp.where(onehot, logits[:, None, :], 0.0), axis=2)
    gate_vals = jax.nn.softmax(picked, axis=-1)
    slot_ids = slot_numbers(routes, priority[0], usable)
    kept_mask = usable[:, None] & (slot_ids < CAP)
    slot_total = EXPERTS * CAP
    flat_dest = jnp.where(kept_mask, routes * CAP + slot_ids, slot_total)
    token_of_slot = (
        jnp.full((slot_total + 1,), row_count, jnp.int32)
        .at[flat_dest.reshape(-1)]
        .set(jnp.repeat(positions, 2))
    )
    token_of_slot = token_of_slot[:slot_total]
    padded_rows = jnp.concatenate([packed_two, jnp.zeros((1, D), jnp.bfloat16)], axis=0)
    send_rows = jnp.take(padded_rows, token_of_slot, axis=0).reshape(EXPERTS, CAP, D)
    arrived = lax.all_to_all(send_rows, "expert", split_axis=0, concat_axis=1, tiled=True)
    arrived = lax.all_gather(arrived, "dp", axis=1, tiled=True)
    hidden = jnp.einsum("erd,edf->erf", arrived, up_slice, preferred_element_type=jnp.float32)
    activated, gelu_pull = jax.vjp(partial(jax.nn.gelu, approximate=False), hidden)
    activated = activated.astype(jnp.bfloat16)
    produced = jnp.einsum(
        "erf,efd->erd", activated, w_down, preferred_element_type=jnp.float32
    ).astype(jnp.bfloat16)
    produced = lax.psum_scatter(produced, "dp", scatter_dimension=1, tiled=True)
    returned = lax.all_to_all(produced, "expert", split_axis=1, concat_axis=0, tiled=True)
    flat_back = jnp.concatenate(
        [returned.reshape(slot_total, D), jnp.zeros((1, D), jnp.bfloat16)], axis=0
    )
    first_back = jnp.take(flat_back, flat_dest[:, 0], axis=0).astype(jnp.float32)
    second_back = jnp.take(flat_back, flat_dest[:, 1], axis=0).astype(jnp.float32)
    result = middle + gate_vals[:, 0:1] * first_back + gate_vals[:, 1:2] * second_back
    out_tokens = result.astype(jnp.bfloat16)
    grad_rows = out_grad.astype(jnp.float32)
    gate_grad = jnp.stack(
        [jnp.sum(grad_rows * first_back, axis=1), jnp.sum(grad_rows * second_back, axis=1)], axis=1
    )
    picked_grad = gate_vals * (gate_grad - jnp.sum(gate_vals * gate_grad, axis=1, keepdims=True))
    logit_grad = jnp.sum(jnp.where(onehot, picked_grad[:, :, None], 0.0), axis=1)
    slot_gate = (
        jnp.zeros((slot_total + 1,), jnp.float32)
        .at[flat_dest.reshape(-1)]
        .set(gate_vals.reshape(-1))
    )
    grad_pad = jnp.concatenate([grad_rows, jnp.zeros((1, D), jnp.float32)], axis=0)
    grad_send = (jnp.take(grad_pad, token_of_slot, axis=0) * slot_gate[:slot_total, None]).astype(
        jnp.bfloat16
    )
    grad_arrived = lax.all_to_all(
        grad_send.reshape(EXPERTS, CAP, D), "expert", split_axis=0, concat_axis=1, tiled=True
    )
    grad_arrived = lax.all_gather(grad_arrived, "dp", axis=1, tiled=True)
    down_share = jnp.einsum(
        "erf,erd->efd", activated, grad_arrived, preferred_element_type=jnp.float32
    )
    acted_grad = jnp.einsum(
        "erd,efd->erf", grad_arrived, w_down, preferred_element_type=jnp.float32
    )
    hidden_grad = gelu_pull(acted_grad)[0].astype(jnp.bfloat16)
    up_grad = jnp.einsum("erd,erf->edf", arrived, hidden_grad, preferred_element_type=jnp.float32)
    up_share = lax.all_to_all(
        up_grad.astype(jnp.bfloat16), "dp", split_axis=1, concat_axis=2, tiled=True
    ).astype(jnp.float32)
    input_grad = jnp.einsum(
        "erf,edf->erd", hidden_grad, up_slice, preferred_element_type=jnp.float32
    ).astype(jnp.bfloat16)
    input_grad = lax.psum_scatter(input_grad, "dp", scatter_dimension=1, tiled=True)
    back_grad = lax.all_to_all(input_grad, "expert", split_axis=1, concat_axis=0, tiled=True)
    flat_grad = jnp.concatenate(
        [back_grad.reshape(slot_total, D), jnp.zeros((1, D), jnp.bfloat16)], axis=0
    )
    normed_two_grad = jnp.take(flat_grad, flat_dest[:, 0], axis=0).astype(jnp.float32)
    normed_two_grad = normed_two_grad + jnp.take(flat_grad, flat_dest[:, 1], axis=0).astype(
        jnp.float32
    )
    normed_two_grad = normed_two_grad + jnp.einsum(
        "te,de->td", logit_grad, router_f32, precision=lax.Precision.HIGHEST
    )
    router_grad = jnp.einsum("td,te->de", packed_f32, logit_grad, precision=lax.Precision.HIGHEST)
    middle_part, gain_two_grad, shift_two_grad = pull_two(normed_two_grad)
    middle_grad = grad_rows + middle_part
    branch_grad = middle_grad.astype(jnp.bfloat16)
    out_proj_grad = jnp.einsum(
        "td,te->de", mixed_rows, branch_grad, preferred_element_type=jnp.float32
    )
    mixed_grad = jnp.einsum(
        "te,de->td", branch_grad, outp_full, preferred_element_type=jnp.float32
    ).astype(jnp.bfloat16)
    grad_blocks = mixed_grad.reshape(blocks, PATCH_L, HEADS, HEAD_DIM)

    def backward_block(carried, operands):
        key_acc, value_acc = carried
        query_blk, seg_blk, grad_blk = operands
        attn_probs = block_probs(query_blk, seg_blk, key_rows, segment_ids)
        probs_grad = jnp.einsum(
            "qhc,khc->hqk", grad_blk, value_rows, preferred_element_type=jnp.float32
        )
        value_acc = value_acc + jnp.einsum(
            "hqk,qhc->khc",
            attn_probs.astype(jnp.bfloat16),
            grad_blk,
            preferred_element_type=jnp.float32,
        )
        score_grad = attn_probs * (
            probs_grad - jnp.sum(attn_probs * probs_grad, axis=-1, keepdims=True)
        )
        raw_grad = (score_grad * scale_factor).astype(jnp.bfloat16)
        query_grad = jnp.einsum(
            "hqk,khc->qhc", raw_grad, key_rows, preferred_element_type=jnp.float32
        )
        key_acc = key_acc + jnp.einsum(
            "hqk,qhc->khc", raw_grad, query_blk, preferred_element_type=jnp.float32
        )
        return ((key_acc, value_acc), query_grad)

    zero_heads = jnp.zeros((row_count, HEADS, HEAD_DIM), jnp.float32)
    (key_grad, value_grad), query_grads = lax.scan(
        backward_block, (zero_heads, zero_heads), (query_blocks, seg_blocks, grad_blocks)
    )
    projected_grad = jnp.concatenate(
        [
            query_grads.reshape(row_count, D),
            key_grad.reshape(row_count, D),
            value_grad.reshape(row_count, D),
        ],
        axis=1,
    ).astype(jnp.bfloat16)
    qkv_grad = jnp.einsum(
        "td,te->de", packed_one, projected_grad, preferred_element_type=jnp.float32
    )
    normed_one_grad = jnp.einsum(
        "te,de->td", projected_grad, qkv_full, preferred_element_type=jnp.float32
    )
    rows_part, gain_one_grad, shift_one_grad = pull_one(normed_one_grad)
    tokens_grad = middle_grad + rows_part
    dense_grad = jnp.concatenate(
        [qkv_grad, out_proj_grad, router_grad]
        + [
            vector[:, None]
            for vector in (gain_one_grad, shift_one_grad, gain_two_grad, shift_two_grad)
        ],
        axis=1,
    ).astype(jnp.bfloat16)
    dense_share = lax.psum_scatter(dense_grad, every, scatter_dimension=0, tiled=True).astype(
        jnp.float32
    )
    return (
        out_tokens,
        tokens_grad,
        dense_share[:, edges[2]],
        dense_share[:, edges[2] + 1],
        dense_share[:, : edges[0]],
        dense_share[:, edges[0] : edges[1]],
        dense_share[:, edges[2] + 2],
        dense_share[:, edges[2] + 3],
        dense_share[:, edges[1] : edges[2]],
        up_share,
        down_share,
    )


def solution(mesh):
    placed = (
        P(("dp", "expert"), None),
        P(("dp", "expert"), None),
        P(("dp", "expert"), None),
        P(("dp", "expert"), None),
        P(("dp", "expert"), None),
        P(("dp", "expert")),
        P(("dp", "expert")),
        P(("dp", "expert"), None),
        P(("dp", "expert"), None),
        P(("dp", "expert")),
        P(("dp", "expert")),
        P(("dp", "expert"), None),
        P("expert", "dp", None),
        P("expert", "dp", None),
    )
    return jax.shard_map(
        body,
        mesh=mesh,
        in_specs=placed,
        out_specs=(
            P(("dp", "expert"), None),
            P(("dp", "expert"), None),
            P(("dp", "expert")),
            P(("dp", "expert")),
            P(("dp", "expert"), None),
            P(("dp", "expert"), None),
            P(("dp", "expert")),
            P(("dp", "expert")),
            P(("dp", "expert"), None),
            P("expert", "dp", None),
            P("expert", "dp", None),
        ),
        check_vma=False,
    )
```
